256 devices in a mesh: req: 64 (over x, z, core), tensor: 4 (over y).
Axes of the slice: x: 4, y: 4, z: 8, core: 2. Of those that a mesh axis runs over, the one named last changes fastest.
Arguments:
- stream: bfloat16 [65536, 2048], P('req', 'tensor'), may hold values from -64 to 64
- target_row: int32 [65536], P('req'), may hold values from -1 to 65535, as said below
- segment_ids: int32 [65536], P('req'), may hold values from -1 to 63, as said below
- cache_slot: int32 [65536], P('req'), may hold values from -1 to 2047, as said below
- norm_gain: bfloat16 [2048], replicated, may hold values from 0.099609375 to 1.8984375
- norm_bias: bfloat16 [2048], replicated, may hold values from -3 to 3
- projection: bfloat16 [2048, 3, 2048], P(None, None, 'tensor'), may hold values from -1 to 1
- output_weight: bfloat16 [2048, 2048], P('tensor'), may hold values from -0.125 to 0.125
- cache_pool: bfloat16 [131072, 2, 2048], P('req', None, 'tensor'), may hold values from -6 to 6
Outputs:
- mixed: bfloat16 [65536, 2048], P('req', 'tensor')
- new_pool: bfloat16 [131072, 2, 2048], P('req', None, 'tensor')
The draws below stay inside these ranges and needn't reach their ends.
Inputs may be any that keep to these rules, and one draw needn't show every extreme that they name: `target_row`: every live row of the request layout is named by exactly one stream row and no other row is named. A device names at most 16 rows of any one device; in every draw some device receives exactly 16 rows from every device and its 1024 rows are all live. `segment_ids`: within one device's 1024 rows the numbers start at 0 on the first row, rise by one at each new request and never fall; a request's rows are consecutive and never cross devices; -1 only on the rows after the last request. A device holds at most 64 requests, and in every draw some device holds exactly that many. `cache_slot`: live rows of one device have distinct slots; a request's rows fill its pages in order, each page being 16 consecutive slots beginning at a multiple of 16; -1 exactly on rows where segment_ids is -1.
All inputs are finite; a program needn't handle non-finite values.
Results may differ from the reference program's by a relative error of at most 0.008.
Values may be sent and summed in bfloat16 or wider, within the bound.
No kernel may reach another device: no remote copies, remote signals or barrier semaphores. Data moves between devices by JAX's collectives and lax.ppermute only.
A program may use at most 128 MiB of HBM per device.

```python
import math
import jax
import jax.numpy as jnp
from jax import lax

D = 2048
HEADS = 8
HDIM = 256
ROT = 64
PAGE = 16
TOK_DEV = 1024
POOL_ROWS = 2048
TOKENS = 65536
N_REQ = 64
N_TENSOR = 4


def layout_tables(key):
    subkeys = jax.random.split(jax.random.fold_in(key, 17), 8)
    cap_rows = TOK_DEV // N_REQ
    device_ids = jnp.arange(N_REQ, dtype=jnp.int32)
    row_ids = jnp.arange(TOK_DEV, dtype=jnp.int32)
    used_rows = jax.random.randint(subkeys[0], (N_REQ,), 2 * TOK_DEV // 5, TOK_DEV + 1)
    full_device = jax.random.randint(subkeys[1], (), 0, N_REQ)
    used_rows = jnp.where((device_ids == full_device) | (device_ids == N_REQ - 1), TOK_DEV, used_rows)
    is_live = row_ids[None, :] < used_rows[:, None]
    window = row_ids // PAGE
    start_offset = jax.random.randint(subkeys[2], (N_REQ, TOK_DEV // PAGE), 0, PAGE)
    start_offset = start_offset.at[:, 0].set(0)
    opens = jax.random.randint(subkeys[3], (N_REQ, TOK_DEV // PAGE), 0, 8) == 0
    opens = opens | (device_ids == full_device)[:, None]
    opens = opens.at[:, 0].set(True)
    candidate = (row_ids % PAGE)[None, :] == start_offset[:, window]
    is_start = candidate & opens[:, window] & is_live
    segment = jnp.where(is_live, jnp.cumsum(is_start.astype(jnp.int32), axis=1) - 1, -1)
    first_row = lax.cummax(jnp.where(is_start, row_ids[None, :], 0), axis=1)
    position = row_ids[None, :] - first_row
    page_start = (is_live & (position % PAGE == 0)).astype(jnp.int32)
    page_index = jnp.maximum(jnp.cumsum(page_start, axis=1) - 1, 0)
    page_order = jax.vmap(lambda subkey: jax.random.permutation(subkey, POOL_ROWS // PAGE))(jax.random.split(subkeys[4], N_REQ))
    slot = jnp.take_along_axis(page_order.astype(jnp.int32), page_index.astype(jnp.int32), axis=1) * PAGE + position % PAGE
    slot = jnp.where(is_live, slot, -1)
    offsets = jax.random.permutation(subkeys[5], N_REQ).astype(jnp.int32)
    slot_order = jax.vmap(lambda subkey: jax.random.permutation(subkey, TOK_DEV))(jax.random.split(subkeys[6], N_REQ)).astype(jnp.int32)
    slot_inverse = jnp.argsort(slot_order, axis=1).astype(jnp.int32)
    stream_order = jax.vmap(lambda subkey: jax.random.permutation(subkey, TOK_DEV))(jax.random.split(subkeys[7], N_REQ)).astype(jnp.int32)
    block_number = stream_order // cap_rows
    receiver = (device_ids[:, None] - offsets[block_number]) % N_REQ
    dest_local = slot_inverse[receiver, stream_order]
    sends_row = dest_local < used_rows[receiver]
    target = jnp.where(sends_row, receiver * TOK_DEV + dest_local, -1)
    return (segment.astype(jnp.int32), position.astype(jnp.int32), slot.astype(jnp.int32), target.astype(jnp.int32), is_live)


def draw_target_row(key, part):
    tables = layout_tables(key)
    return tables[3].reshape(-1).astype(jnp.int32)


def draw_segment_ids(key, part):
    tables = layout_tables(key)
    return tables[0].reshape(-1).astype(jnp.int32)


def draw_cache_slot(key, part):
    tables = layout_tables(key)
    return tables[2].reshape(-1).astype(jnp.int32)


def draw_stream(key, part):
    subkeys = jax.random.split(jax.random.fold_in(key, 29), 1)
    values = jnp.clip(jax.random.normal(subkeys[0], (TOKENS, D), jnp.float32), -4.0, 4.0)
    return values.astype(jnp.bfloat16)


def draw_projection(key, part):
    subkeys = jax.random.split(jax.random.fold_in(key, 41), 1)
    head_width = HEADS * HDIM
    base = jnp.clip(jax.random.normal(subkeys[0], (D, 3, head_width), jnp.float32), -4.0, 4.0) / math.sqrt(D)
    return jnp.clip(base, -1.0, 1.0).astype(jnp.bfloat16)


def block_levels(own_key, extent, cuts, least, top_value):
    def one(dim, parts):
        draws = jax.random.uniform(jax.random.fold_in(jax.random.fold_in(own_key, 6), dim), (parts,), jnp.float32, least / len(cuts), top_value / len(cuts))
        return jnp.repeat(jnp.exp(draws), extent[dim] // parts).reshape((-1,) + (1,) * (len(extent) - dim - 1))

    gain = one(*cuts[0])
    for cut in cuts[1:]:
        gain = gain * one(*cut)
    return gain


def bell_draw(key, extent, scale, bound, cuts=(), held_as=jnp.bfloat16):
    drawn = scale * jax.random.normal(key, extent, jnp.float32)
    if cuts:
        drawn = drawn * block_levels(key, extent, cuts, -0.22, 0.18)
    return jnp.clip(drawn, -bound, bound).astype(held_as)


def setup_inputs(seed: int = 0) -> dict:
    key_list = jax.random.split(jax.random.key(seed), 10)
    return {
        "stream": draw_stream(jax.random.fold_in(key_list[9], 71), 0),
        "target_row": draw_target_row(jax.random.fold_in(key_list[9], 71), 0),
        "segment_ids": draw_segment_ids(jax.random.fold_in(key_list[9], 71), 0),
        "cache_slot": draw_cache_slot(jax.random.fold_in(key_list[9], 71), 0),
        "norm_gain": jnp.clip(1.0 + 0.18 * jax.random.normal(key_list[4], (D,), jnp.float32), 0.099609375, 1.8984375).astype(jnp.bfloat16),
        "norm_bias": bell_draw(key_list[5], (D,), 0.5, 3.0),
        "projection": draw_projection(jax.random.fold_in(key_list[9], 71), 0),
        "output_weight": bell_draw(key_list[7], (HEADS * HDIM, D), (HEADS * HDIM) ** -0.5, 0.125, ((0, 4),)),
        "cache_pool": bell_draw(key_list[8], (N_REQ * POOL_ROWS, 2, HEADS * HDIM), 1.0, 6.0, ((0, 64), (2, 4))),
    }


norm_epsilon = 1e-05
masked_score = -1e+30
rotary_base = 10000.0

def layer_norm(values, norm_gain, norm_bias):
    widened = values.astype(jnp.float32)
    row_mean = lax.optimization_barrier(jnp.mean(widened, axis=-1, keepdims=True))
    centred = widened - row_mean
    row_var = lax.optimization_barrier(jnp.mean(centred * centred, axis=-1, keepdims=True))
    scaled = centred * lax.rsqrt(row_var + norm_epsilon)
    return (scaled * norm_gain.astype(jnp.float32) + norm_bias.astype(jnp.float32)).astype(jnp.bfloat16)

def positions(segment):
    row_ids = jnp.arange(segment.shape[0], dtype=jnp.int32)
    earlier = jnp.concatenate([jnp.full((1,), -2, jnp.int32), segment[:-1].astype(jnp.int32)])
    is_start = segment.astype(jnp.int32) != earlier
    first_row = lax.cummax(jnp.where(is_start, row_ids, 0), axis=0)
    return row_ids - first_row

def rotary(heads_in, position):
    half_rot = ROT // 2
    exponent = jnp.arange(half_rot, dtype=jnp.float32) * (2.0 / ROT)
    inverse_freq = 1.0 / rotary_base ** exponent
    angles = position.astype(jnp.float32)[:, None] * inverse_freq[None, :]
    cosine = jnp.cos(angles)[:, None, :]
    sine_part = jnp.sin(angles)[:, None, :]
    widened = heads_in.astype(jnp.float32)
    row_count = widened.shape[0]
    head_count = widened.shape[1]
    paired = widened[..., :ROT].reshape(row_count, head_count, half_rot, 2)
    even_part = paired[..., 0]
    odd_part = paired[..., 1]
    turned = jnp.stack([even_part * cosine - odd_part * sine_part, odd_part * cosine + even_part * sine_part], axis=-1)
    turned = turned.reshape(row_count, head_count, ROT)
    return jnp.concatenate([turned, widened[..., ROT:]], axis=-1).astype(jnp.bfloat16)

def device_layer(placed, segment, slots, pool_part, norm_gain, norm_bias, projection, output_weight):
    row_count = placed.shape[0]
    head_width = HEADS * HDIM
    score_scale = 1.0 / math.sqrt(HDIM)
    is_live = segment >= 0
    position = positions(segment)
    normed = layer_norm(placed, norm_gain, norm_bias)
    projected = jnp.dot(normed, projection.reshape(D, 3 * head_width), preferred_element_type=jnp.float32).astype(jnp.bfloat16)
    projected = projected.reshape(row_count, 3, HEADS, HDIM)
    queries = rotary(projected[:, 0], position)
    keys_rot = rotary(projected[:, 1], position)
    values_all = projected[:, 2]
    scores = jnp.einsum('qhd,khd->hqk', queries.astype(jnp.float32), keys_rot.astype(jnp.float32)) * score_scale
    row_ids = jnp.arange(row_count, dtype=jnp.int32)
    allowed = (segment[:, None] == segment[None, :]) & (row_ids[None, :] <= row_ids[:, None])
    scores = jnp.where(allowed[None], scores, masked_score)
    top_score = lax.optimization_barrier(jnp.max(scores, axis=-1, keepdims=True))
    raised = jnp.where(allowed[None], jnp.exp(scores - top_score), 0.0)
    row_total = lax.optimization_barrier(jnp.sum(raised, axis=-1, keepdims=True))
    weights = (raised / row_total).astype(jnp.bfloat16)
    context = jnp.einsum('hqk,khd->qhd', weights.astype(jnp.float32), values_all.astype(jnp.float32)).astype(jnp.bfloat16)
    grouped = context.reshape(row_count, N_TENSOR, head_width // N_TENSOR).astype(jnp.float32)
    out_groups = output_weight.reshape(N_TENSOR, head_width // N_TENSOR, D).astype(jnp.float32)
    head_partial = jnp.einsum('tgf,gfd->gtd', grouped, out_groups).astype(jnp.bfloat16)
    head_partial = lax.optimization_barrier(head_partial)
    summed = lax.optimization_barrier(jnp.sum(head_partial.astype(jnp.float32), axis=0))
    mixed_rows = jnp.where(is_live[:, None], placed.astype(jnp.float32) + summed, 0.0).astype(jnp.bfloat16)
    key_value = jnp.stack([keys_rot.reshape(row_count, head_width), values_all.reshape(row_count, head_width)], axis=1)
    where_slot = jnp.where(is_live, slots, pool_part.shape[0])
    new_pool = pool_part.at[where_slot].set(key_value, mode='drop')
    return (mixed_rows, new_pool)

def reference(stream, target_row, segment_ids, cache_slot, norm_gain, norm_bias, projection, output_weight, cache_pool):
    head_width = HEADS * HDIM
    where_to = jnp.where(target_row >= 0, target_row, TOKENS)
    placed = jnp.zeros((TOKENS, D), jnp.bfloat16).at[where_to].set(stream, mode='drop')

    def one_device(packed):
        return device_layer(packed[0], packed[1], packed[2], packed[3], norm_gain, norm_bias, projection, output_weight)
    mixed_rows, new_pool = lax.map(one_device, (placed.reshape(N_REQ, TOK_DEV, D), segment_ids.reshape(N_REQ, TOK_DEV), cache_slot.reshape(N_REQ, TOK_DEV), cache_pool.reshape(N_REQ, POOL_ROWS, 2, head_width)))
    return (mixed_rows.reshape(TOKENS, D), new_pool.reshape(N_REQ * POOL_ROWS, 2, head_width))
```

```python
import functools
import math

import jax
import jax.numpy as jnp
from jax import lax
from jax.experimental import pallas as pl
from jax.experimental.pallas import tpu as pltpu
from jax.sharding import PartitionSpec as P

HDIM = 256
ROT = 64
LANES = 128
BLOCK = 256
CHUNKS = 2


norm_epsilon = 1e-05
masked_score = -1e30
rotary_base = 10000.0


def layer_norm(values, norm_gain, norm_bias):
    widened = values.astype(jnp.float32)
    row_mean = jnp.mean(widened, axis=-1, keepdims=True)
    centred = widened - row_mean
    row_var = jnp.mean(centred * centred, axis=-1, keepdims=True)
    scaled = centred * lax.rsqrt(row_var + norm_epsilon)
    return (scaled * norm_gain.astype(jnp.float32) + norm_bias.astype(jnp.float32)).astype(
        jnp.bfloat16
    )


def rotary_tables(position):
    lane = jnp.arange(LANES, dtype=jnp.int32)
    exponent = (lane // 2).astype(jnp.float32) * (2.0 / ROT)
    inverse_freq = 1.0 / rotary_base**exponent
    angles = position.astype(jnp.float32)[:, None] * inverse_freq[None, :]
    turned = (lane < ROT)[None, :]
    even = (lane % 2 == 0)[None, :]
    sine = jnp.where(turned, jnp.sin(angles), 0.0)
    same = jnp.where(turned, jnp.cos(angles), 1.0)
    return same, jnp.where(even, -sine, 0.0), jnp.where(even, 0.0, sine)


def attention_kernel(prev_count, chunk, q_ref, k_ref, v_ref, same_ref, ahead_ref, behind_ref,
                     segq_ref, segk_ref, *rest):
    prev_keys = rest[:prev_count]
    prev_values = rest[prev_count : 2 * prev_count]
    ctx_ref, key_ref, scratch = rest[2 * prev_count :]
    block = pl.program_id(1)
    blocks = scratch.shape[0]
    same = same_ref[...]
    ahead = ahead_ref[...]
    behind = behind_ref[...]

    def turn(x):
        low = x[:, :LANES].astype(jnp.float32)
        low = (
            low * same
            + pltpu.roll(low, LANES - 1, 1) * ahead
            + pltpu.roll(low, 1, 1) * behind
        )
        return jnp.concatenate([low.astype(jnp.bfloat16), x[:, LANES:]], axis=1)

    queries = turn(q_ref[...])
    new_keys = turn(k_ref[...])
    key_ref[...] = new_keys
    scratch[block] = new_keys
    seg_q = segq_ref[...]
    chunk_rows = blocks * BLOCK

    def run(inner):
        pieces = []
        for n in range(prev_count):
            pieces.append((prev_keys[n][...], prev_values[n][...], n * chunk_rows, chunk_rows, False))
        for n in range(inner + 1):
            pieces.append((scratch[n], v_ref[n * BLOCK : (n + 1) * BLOCK, :],
                           chunk * chunk_rows + n * BLOCK, BLOCK, n == inner))
        scored = []
        for keys, values, start, size, diagonal in pieces:
            raw = lax.dot_general(queries, keys, (((1,), (1,)), ((), ())),
                                  preferred_element_type=jnp.float32) * (1.0 / math.sqrt(HDIM))
            allowed = seg_q == segk_ref[:, start : start + size]
            if diagonal:
                allowed &= lax.broadcasted_iota(jnp.int32, raw.shape, 1) <= lax.broadcasted_iota(
                    jnp.int32, raw.shape, 0)
            scored.append(jnp.where(allowed, raw, masked_score))
        top = functools.reduce(jnp.maximum, [jnp.max(s, axis=1, keepdims=True) for s in scored])
        total = 0.0
        context = 0.0
        for s, piece in zip(scored, pieces):
            raised = jnp.exp(s - top)
            total = total + jnp.sum(raised, axis=1, keepdims=True)
            context = context + jnp.dot(raised.astype(jnp.bfloat16), piece[1],
                                        preferred_element_type=jnp.float32)
        ctx_ref[...] = (context / total).astype(jnp.bfloat16)

    for inner in range(blocks):
        pl.when(block == inner)(functools.partial(run, inner))


def attention(chunk, projected, keys, tables, seg_col, seg_row):
    current = projected[chunk]
    rows = current.shape[0]
    heads = current.shape[1] // (3 * HDIM)
    blocks = rows // BLOCK
    tile = lambda column: pl.BlockSpec((BLOCK, HDIM), lambda h, b: (b, column * heads + h))
    table = pl.BlockSpec((BLOCK, LANES), lambda h, b: (chunk * blocks + b, 0))
    values = pl.BlockSpec((rows, HDIM), lambda h, b: (0, 2 * heads + h))
    whole = pl.BlockSpec((rows, HDIM), lambda h, b: (0, h))
    out = jax.ShapeDtypeStruct((rows, heads * HDIM), jnp.bfloat16)
    return pl.pallas_call(
        functools.partial(attention_kernel, chunk, chunk),
        grid=(heads, blocks),
        in_specs=[tile(0), tile(1), values, table, table, table,
                  pl.BlockSpec((BLOCK, 1), lambda h, b: (chunk * blocks + b, 0)),
                  pl.BlockSpec(seg_row.shape, lambda h, b: (0, 0))]
        + [whole] * chunk + [values] * chunk,
        out_specs=[pl.BlockSpec((BLOCK, HDIM), lambda h, b: (b, h))] * 2,
        out_shape=[out, out],
        scratch_shapes=[pltpu.VMEM((blocks, BLOCK, HDIM), jnp.bfloat16)],
        name="attend",
    )(current, current, current, *tables, seg_col, seg_row, *keys, *projected[:chunk])


def shards(
    stream,
    target_row,
    segment_ids,
    cache_slot,
    norm_gain,
    norm_bias,
    projection,
    output_weight,
    cache_pool,
):
    peer_count = lax.axis_size("req")
    own = lax.axis_index("req")
    row_count, width = stream.shape
    cap_rows = row_count // peer_count
    chunk_rows = row_count // CHUNKS
    row_ids = jnp.arange(row_count, dtype=jnp.int32)
    slot_ids = jnp.arange(peer_count * cap_rows, dtype=jnp.int32)
    earlier = (row_ids[:, None] < row_ids[None, :]).astype(jnp.bfloat16)

    all_targets = lax.all_gather(target_row, "req", axis=0, tiled=False)

    sends_row = target_row >= 0
    receiver = jnp.where(sends_row, target_row // row_count, peer_count)
    onehot = (jnp.arange(peer_count, dtype=jnp.int32)[:, None] == receiver[None, :])
    before = jnp.dot(onehot.astype(jnp.bfloat16), earlier, preferred_element_type=jnp.float32)
    rank = jnp.sum(jnp.where(onehot, before, 0.0), axis=0).astype(jnp.int32)
    send_slot = jnp.where(sends_row, receiver * cap_rows + rank, -1)
    send_matrix = (slot_ids[:, None] == send_slot[None, :]).astype(jnp.bfloat16)
    packed = jnp.dot(send_matrix, stream, preferred_element_type=jnp.float32).astype(jnp.bfloat16)
    arrived = lax.all_to_all(
        packed.reshape(peer_count, cap_rows, width), "req", split_axis=0, concat_axis=0, tiled=True
    ).reshape(peer_count * cap_rows, width)

    mine = (all_targets >= 0) & (all_targets // row_count == own)
    mine_before = jnp.dot(mine.astype(jnp.bfloat16), earlier, preferred_element_type=jnp.float32)
    mine_rank = jnp.where(mine, mine_before.astype(jnp.int32), -1)
    mine_row = all_targets % row_count + 1
    slot_of_peer = jnp.arange(cap_rows, dtype=jnp.int32)
    arrived_rows = jnp.sum(
        jnp.where(
            mine_rank[:, None, :] == slot_of_peer[None, :, None], mine_row[:, None, :], 0
        ),
        axis=2,
    ).reshape(-1) - 1
    place_matrix = (row_ids[:, None] == arrived_rows[None, :]).astype(jnp.bfloat16)

    is_live = segment_ids >= 0
    position = (
        jnp.sum(
            (
                (segment_ids[:, None] == segment_ids[None, :])
                & (row_ids[None, :] <= row_ids[:, None])
            ).astype(jnp.int32),
            axis=1,
        )
        - 1
    )
    tables = rotary_tables(position)
    seg_col = segment_ids[:, None]
    seg_row = segment_ids[None, :]
    flat_weight = projection.reshape(projection.shape[0], projection.shape[1] * projection.shape[2])

    placed = jnp.dot(place_matrix, arrived, preferred_element_type=jnp.float32).astype(jnp.bfloat16)
    gathered = []
    for c in range(CHUNKS):
        part = placed[c * chunk_rows : (c + 1) * chunk_rows]
        gathered.append(lax.all_gather(part, "tensor", axis=1, tiled=True))

    projected = []
    keys = []
    summed = []
    for c in range(CHUNKS):
        features = gathered[c]
        if c:
            features, _ = lax.optimization_barrier((features, head_partial))
        normed = layer_norm(features, norm_gain, norm_bias)
        projected.append(
            jnp.dot(normed, flat_weight, preferred_element_type=jnp.float32).astype(jnp.bfloat16)
        )
        context, new_keys = attention(c, projected, keys, tables, seg_col, seg_row)
        keys.append(new_keys)
        head_partial = jnp.dot(
            context, output_weight, preferred_element_type=jnp.float32
        ).astype(jnp.bfloat16)
        summed.append(lax.psum_scatter(head_partial, "tensor", scatter_dimension=1, tiled=True))

    total = jnp.concatenate(summed, axis=0).astype(jnp.float32)
    mixed_rows = jnp.where(is_live[:, None], placed.astype(jnp.float32) + total, 0.0).astype(
        jnp.bfloat16
    )

    pool_ids = jnp.arange(cache_pool.shape[0], dtype=jnp.int32)
    live_slot = jnp.where(is_live, cache_slot, -1)
    pool_hit = pool_ids[:, None] == live_slot[None, :]
    pool_found = jnp.any(pool_hit, axis=1)
    pool_matrix = pool_hit.astype(jnp.bfloat16)
    key_rows = jnp.concatenate(keys, axis=0)
    value_rows = jnp.concatenate([p[:, 2 * width :] for p in projected], axis=0)
    pool_keys = jnp.dot(pool_matrix, key_rows, preferred_element_type=jnp.float32)
    pool_values = jnp.dot(pool_matrix, value_rows, preferred_element_type=jnp.float32)
    written = jnp.stack([pool_keys.astype(jnp.bfloat16), pool_values.astype(jnp.bfloat16)], axis=1)
    new_pool = jnp.where(pool_found[:, None, None], written, cache_pool)
    return (mixed_rows, new_pool)


def solution(mesh):
    in_specs = (
        P("req", "tensor"),
        P("req"),
        P("req"),
        P("req"),
        P(),
        P(),
        P(None, None, "tensor"),
        P("tensor", None),
        P("req", None, "tensor"),
    )
    out_specs = (P("req", "tensor"), P("req", None, "tensor"))
    return jax.shard_map(shards, mesh=mesh, in_specs=in_specs, out_specs=out_specs, check_vma=False)
```
